256 devices in a mesh: leaf: 32 (over x, y, core), col: 8 (over z).
Axes of the slice: x: 4, y: 4, z: 8, core: 2. Of those that a mesh axis runs over, the one named last changes fastest.
Arguments:
- near: float32 [512, 13, 256, 256], P(('leaf', 'col')), may hold values from -1 to 6, as said below
- basis: float32 [512, 256, 256], P(('leaf', 'col')), may hold values from -1 to 2
- parent_basis: float32 [128, 256, 256], P('leaf'), may hold values from -1 to 2
- grand_basis: float32 [32, 256, 256], P('leaf'), may hold values from -1 to 2
- nbr: int32 [512, 13], P(('leaf', 'col')), may hold values from 0 to 511, as said below
- live: int32 [512, 13], P(('leaf', 'col')), may hold values from 0 to 1, as said below
- partner: int32 [512, 13], P(('leaf', 'col')), may hold values from 0 to 12, as said below
Outputs:
- leaf_schur: float32 [512, 64, 832], P(('leaf', 'col'))
- parent_schur: float32 [128, 64, 256], P('leaf')
- top_schur: float32 [32, 64, 64], P('leaf')
The draws below stay inside these ranges and needn't reach their ends.
Inputs may be any that keep to these rules, and one draw needn't show every extreme that they name: nbr[j,0] is j; the other 12 slots name distinct leaves at distances 1 to 6 from j in leaf order, taken around the cycle of 512 leaves, in an order drawn per leaf. Slot 0 and the slots of leaves of the same group of four are always 1; live at (nbr[j,k], partner[j,k]) equals live[j,k]; some leaf has all 13 slots 1. nbr[nbr[j,k], partner[j,k]] is j; partner[j,0] is 0. near holds blocks of one symmetric matrix: the block at (nbr[j,k], partner[j,k]) is the transpose of near[j,k], and near[j,0] is symmetric positive definite.
All inputs are finite; a program needn't handle non-finite values.
Results may differ from the reference program's by a relative error of at most 0.000078.
Values sent between devices are 32-bit elements; how exact they have to be, the bound alone decides.
A program may use at most 128 MiB of HBM per device.

```python
import jax
import jax.numpy as jnp
from jax import lax

M = 256
SK = 64
NB = 13
REACH = 6
LEAVES = 512
PARENTS = 128
GRANDS = 32


def draw_noise(noise_key, dims_wanted):
    return jax.random.truncated_normal(noise_key, -4.0, 4.0, dims_wanted, jnp.float32)


def graph_parts(key):
    graph_key = jax.random.fold_in(key, 9001)
    perm_key, edge_key, hub_key = jax.random.split(graph_key, 3)
    offsets_all = jnp.concatenate([jnp.arange(-REACH, 0, dtype=jnp.int32), jnp.arange(1, REACH + 1, dtype=jnp.int32)])
    orders = jax.vmap(lambda one_key: jax.random.permutation(one_key, 2 * REACH))(jax.random.split(perm_key, LEAVES)).astype(jnp.int32)
    slot_offset = offsets_all[orders]
    leaf_ids = jnp.arange(LEAVES, dtype=jnp.int32)
    distance = jnp.arange(1, REACH + 1, dtype=jnp.int32)
    ahead_ids = (leaf_ids[:, None] + distance[None, :]) % LEAVES
    edge_bits = jax.random.randint(edge_key, (LEAVES, REACH), 0, 2, dtype=jnp.int32)
    hub_leaf = jax.random.randint(hub_key, (), 0, LEAVES, dtype=jnp.int32)
    forced = (leaf_ids[:, None] // 4 == ahead_ids // 4) | (leaf_ids[:, None] == hub_leaf) | (ahead_ids == hub_leaf)
    edge_bits = jnp.where(forced, 1, edge_bits)
    others = (leaf_ids[:, None] + slot_offset) % LEAVES
    lower_ids = jnp.where(slot_offset > 0, leaf_ids[:, None], others)
    live_rest = edge_bits[lower_ids, jnp.abs(slot_offset) - 1]
    inverse = jnp.argsort(orders, axis=1).astype(jnp.int32)
    mirror = -slot_offset
    mirror_index = jnp.where(mirror < 0, mirror + REACH, mirror + REACH - 1)
    partner_rest = inverse[others, mirror_index] + 1
    nbr = jnp.concatenate([leaf_ids[:, None], others], axis=1).astype(jnp.int32)
    live = jnp.concatenate([jnp.ones((LEAVES, 1), jnp.int32), live_rest], axis=1).astype(jnp.int32)
    partner = jnp.concatenate([jnp.zeros((LEAVES, 1), jnp.int32), partner_rest], axis=1).astype(jnp.int32)
    return (nbr, live, partner, slot_offset)


def draw_nbr(key, part):
    return graph_parts(key)[0]


def draw_live(key, part):
    return graph_parts(key)[1]


def draw_partner(key, part):
    return graph_parts(key)[2]


def draw_near(key, part):
    nbr, live, partner, slot_offset = graph_parts(key)
    leaf_ids = jnp.arange(LEAVES, dtype=jnp.int32)
    diag_key, off_key = jax.random.split(jax.random.fold_in(key, 17))
    lower_ids = jnp.where(slot_offset > 0, leaf_ids[:, None], nbr[:, 1:])
    edge_id = lower_ids * REACH + jnp.abs(slot_offset) - 1
    flipped = slot_offset > 0

    def one_block(edge_one, flip_one):
        off_block = draw_noise(jax.random.fold_in(off_key, edge_one), (M, M)) * (0.25 / M ** 0.5)
        return jnp.where(flip_one, off_block.T, off_block)
    off_blocks = jax.vmap(jax.vmap(one_block))(edge_id, flipped)
    raw_diag = draw_noise(diag_key, (LEAVES, M, M))
    diag_blocks = 5.0 * jnp.eye(M, dtype=jnp.float32)[None] + (raw_diag + jnp.swapaxes(raw_diag, 1, 2)) / (2.0 * M) ** 0.5
    return jnp.concatenate([diag_blocks[:, None], off_blocks], axis=1).astype(jnp.float32)


def basis_like(key, salt, count):
    raw_part = draw_noise(jax.random.fold_in(key, salt), (count, M, M))
    return (jnp.eye(M, dtype=jnp.float32)[None] + raw_part * (0.2 / M ** 0.5)).astype(jnp.float32)


def draw_basis(key, part):
    return basis_like(key, 23, LEAVES)


def draw_parent_basis(key, part):
    return basis_like(key, 29, PARENTS)


def draw_grand_basis(key, part):
    return basis_like(key, 31, GRANDS)


def setup_inputs(seed: int = 0) -> dict:
    keys = jax.random.split(jax.random.key(seed), 8)
    near = draw_near(jax.random.fold_in(keys[7], 71), 0)
    basis = draw_basis(jax.random.fold_in(keys[7], 71), 0)
    parent_basis = draw_parent_basis(jax.random.fold_in(keys[7], 71), 0)
    grand_basis = draw_grand_basis(jax.random.fold_in(keys[7], 71), 0)
    nbr = draw_nbr(jax.random.fold_in(keys[7], 71), 0)
    live = draw_live(jax.random.fold_in(keys[7], 71), 0)
    partner = draw_partner(jax.random.fold_in(keys[7], 71), 0)
    return {"near": near, "basis": basis, "parent_basis": parent_basis, "grand_basis": grand_basis, "nbr": nbr, "live": live, "partner": partner}


FULL_PRECISION = lax.Precision.HIGHEST

def eliminate(diag_block, columns):
    redundant = diag_block.shape[-1] - SK
    factor = jnp.linalg.cholesky(diag_block[:, :redundant, :redundant])
    solved = jax.scipy.linalg.cho_solve((factor, True), diag_block[:, :redundant, redundant:])
    coupled = jnp.einsum('nrs,nrw->nsw', solved, columns[:, :redundant, :], precision=FULL_PRECISION)
    return (coupled, columns[:, redundant:, :] - coupled)

def parent_level(stacked, own_basis, family, position):
    parents = stacked.shape[0]
    turned = jnp.einsum('nab,nac->nbc', own_basis, stacked, precision=FULL_PRECISION).reshape(parents, M, 4, M)
    chooser = jax.nn.one_hot(position, 4, dtype=jnp.float32)
    own_cols = jnp.einsum('nbqc,nq->nbc', turned, chooser, precision=FULL_PRECISION)
    diag_block = jnp.einsum('nbc,ncd->nbd', own_cols, own_basis, precision=FULL_PRECISION)
    columns = jnp.einsum('nbqc,nqcd->nbqd', turned, family, precision=FULL_PRECISION).reshape(parents, M, 4 * SK)
    return eliminate(diag_block, columns)

def mirror_rows(coupled, remainder):
    grand_count = coupled.shape[0] // 4
    blocks = coupled.reshape(grand_count, 4, SK, 4, SK)
    mirrored = jnp.einsum('gqypx->gpxqy', blocks)
    apart = 1.0 - jnp.eye(4, dtype=jnp.float32)
    result = remainder.reshape(grand_count, 4, SK, 4, SK) - mirrored * apart[None, :, None, :, None]
    return result.reshape(grand_count * 4, SK, 4 * SK)

def top_level(parent_schur, grand_basis):
    joined = parent_schur.reshape(-1, M, M)
    turned = jnp.einsum('gab,gac->gbc', grand_basis, joined, precision=FULL_PRECISION)
    grand_block = jnp.einsum('gbc,gcd->gbd', turned, grand_basis, precision=FULL_PRECISION)
    coupled, remainder = eliminate(grand_block, grand_block[:, :, M - SK:])
    return remainder

def reference(near, basis, parent_basis, grand_basis, nbr, live, partner):
    weights = live.astype(jnp.float32)
    panels = jnp.einsum('jkab,jbc->jkca', near, basis[:, :, M - SK:], precision=FULL_PRECISION) * weights[:, :, None, None]
    fetched = panels[nbr, partner]
    rotated = jnp.einsum('iqca,iab->ibqc', fetched, basis, precision=FULL_PRECISION).reshape(LEAVES, M, NB * SK)
    rows_first = jnp.einsum('iab,iac->ibc', basis, near[:, 0], precision=FULL_PRECISION)
    diag_block = jnp.einsum('ibc,icd->ibd', rows_first, basis, precision=FULL_PRECISION)
    coupled, remainder = eliminate(diag_block, rotated)
    replies = coupled.reshape(LEAVES, SK, NB, SK).transpose(0, 2, 1, 3)
    returned = replies[nbr, partner]
    others = (jnp.arange(NB) > 0).astype(jnp.float32)
    leaf_schur = remainder.reshape(LEAVES, SK, NB, SK) - jnp.einsum('iqba,q->iaqb', returned, others)
    leaf_ids = jnp.arange(LEAVES, dtype=jnp.int32)
    targets = (leaf_ids // 16 * 16)[:, None, None] + jnp.arange(16, dtype=jnp.int32)[None, None, :]
    member = (nbr[:, :, None] == targets).astype(jnp.float32)
    grand_rows = jnp.einsum('iaqb,iqw->iawb', leaf_schur, member, precision=FULL_PRECISION).reshape(LEAVES, SK, 16 * SK)
    stacked = grand_rows.reshape(PARENTS, M, 4 * M)
    family = jnp.repeat(parent_basis[:, :, M - SK:].reshape(GRANDS, 4, M, SK), 4, axis=0)
    position = jnp.arange(PARENTS, dtype=jnp.int32) % 4
    coupled_up, remainder_up = parent_level(stacked, parent_basis, family, position)
    parent_schur = mirror_rows(coupled_up, remainder_up)
    return (leaf_schur.reshape(LEAVES, SK, NB * SK), parent_schur, top_level(parent_schur, grand_basis))
```

```python
import functools

import jax
import jax.numpy as jnp
from jax import lax
from jax.experimental import pallas as pl
from jax.experimental.pallas import tpu as pltpu
from jax.sharding import PartitionSpec as P

M = 256
SK = 64
RD = 192
NB = 13
G = 16
F32 = jnp.float32
HIGH = lax.Precision.HIGH
MESH = pl.DeviceIdType.MESH
NN = ((1,), (0,))
NT = ((1,), (1,))
TN = ((0,), (0,))


def mm(a, b, dims=NN):
    return lax.dot_general(a, b, (dims, ((), ())), precision=HIGH, preferred_element_type=F32)


def lane(x, k):
    return jnp.broadcast_to(x[:, k : k + 1], x.shape)


def sublane(x, k):
    return jnp.broadcast_to(x[k : k + 1, :], x.shape)


def tree_sum(terms):
    while len(terms) > 1:
        terms = [
            terms[i] + terms[i + 1] if i + 1 < len(terms) else terms[i]
            for i in range(0, len(terms), 2)
        ]
    return terms[0]


def forward_steps(rows_all, size, found):
    depth = G // 8
    row_ids = lax.broadcasted_iota(jnp.int32, (8, 128), 0)
    before, after = [], []
    for g in range(size // G):
        top, k0 = depth * g, G * g
        rows = list(rows_all[top : top + depth])
        before += rows
        cols = [[lane(rows[h], k0 + j) for h in range(depth)] for j in range(G)]
        for k in range(G):
            kh, ks = divmod(k, 8)
            inverse = 1.0 / sublane(cols[k][kh], ks)
            pivot_row = sublane(rows[kh], ks) * inverse
            pivot_cols = [
                sublane(cols[j][kh], ks) * inverse if j > k else None for j in range(G)
            ]
            factor = cols[k]
            for h in range(depth):
                for j in range(k + 1, G):
                    value = cols[j][h] - factor[h] * pivot_cols[j]
                    cols[j][h] = (
                        jnp.where(row_ids == ks, pivot_cols[j], value) if h == kh else value
                    )
                value = rows[h] - factor[h] * pivot_row
                rows[h] = jnp.where(row_ids == ks, pivot_row, value) if h == kh else value
            yield
        after += rows
        for u in range(top + depth, size // 8):
            rows_all[u] = rows_all[u] - tree_sum(
                [
                    lane(rows_all[u], k0 + j) * sublane(rows[j // 8], j % 8)
                    for j in range(G)
                ]
            )
    found.append((before, after))


def half_inverses(blocks):
    size = blocks[0].shape[0]
    r = lax.broadcasted_iota(jnp.int32, (size, size), 0)
    c = lax.broadcasted_iota(jnp.int32, (size, size), 1)
    eye = jnp.where(r == c, 1.0, 0.0).astype(F32)
    found, steps = [], []
    for block in blocks:
        wide = jnp.concatenate([block, eye], axis=1)
        mine = []
        found.append(mine)
        steps.append(
            forward_steps([wide[8 * i : 8 * i + 8] for i in range(size // 8)], size, mine)
        )
    going = True
    while going:
        for step in steps:
            if next(step, 0) == 0:
                going = False
    out = []
    for mine in found:
        before, after = mine[0]
        out.append(
            (
                jnp.concatenate(before, axis=0)[:, size:],
                jnp.concatenate(after, axis=0)[:, size:],
            )
        )
    return out


def eliminate(diags, bases, between=None):
    upper = [d[:RD] for d in diags]
    lower = list(bases)
    for b in range(3):
        halves = half_inverses([a[:SK, :SK] for a in upper])
        for i, (before, after) in enumerate(halves):
            a, e = upper[i], lower[i]
            z = mm(after, a[:SK, SK:])
            if b < 2:
                upper[i] = a[SK:, SK:] - mm(mm(a[SK:, :SK], before, NT), z)
            lower[i] = e[:, SK:] - mm(mm(e[:, :SK], before, NT), z)
        if between is not None and b < 2:
            between(b)
    return lower


def kernel(
    n_leaf,
    n_col,
    near_h,
    basis_h,
    pb_h,
    gb_h,
    nbr_s,
    live_s,
    leaf_o,
    par_o,
    top_o,
    near_v,
    basis_v,
    pb_v,
    gb_v,
    window,
    turned,
    weigh,
    sent,
    got,
    own_send,
    own_got,
    ring,
    joint,
    mixed,
    mixed_got,
    parts,
    share,
    shares,
    blocks,
    load_sem,
    s_send,
    s_recv,
    f_send,
    f_recv,
    c_sem,
    m_sem,
    e_send,
    e_recv,
):
    total = n_leaf * n_col
    leaf_total = 2 * total
    row = lax.axis_index("leaf")
    col = lax.axis_index("col")
    me = row * n_col + col
    half = lax.rem(col, 2)
    parent = col // 2

    def place(k):
        n = lax.rem(me + k + total, total)
        return (n // n_col, lax.rem(n, n_col))

    partner = (row, col + 1 - 2 * half)

    loads = [
        pltpu.make_async_copy(basis_h, basis_v, load_sem.at[0]),
        pltpu.make_async_copy(near_h.at[:, 0], near_v.at[:, 0], load_sem.at[1]),
        pltpu.make_async_copy(near_h.at[:, 1:], near_v.at[:, 1:], load_sem.at[2]),
        pltpu.make_async_copy(pb_h, pb_v, load_sem.at[3]),
        pltpu.make_async_copy(gb_h, gb_v, load_sem.at[4]),
    ]
    for load in loads:
        load.start()
    barrier = pltpu.get_barrier_semaphore()
    for k in (1, -1, 2, -2, 3, -3):
        pl.semaphore_signal(barrier, inc=1, device_id=place(k), device_id_type=MESH)
    for k in range(1, n_col):
        pl.semaphore_signal(
            barrier, inc=1, device_id=(row, lax.rem(col + k, n_col)), device_id_type=MESH
        )

    loads[0].wait()
    flipped = []
    for i in range(2):
        t = basis_v[i].T
        flipped.append(t)
        window[3, SK * i : SK * (i + 1), :] = t[RD:, :]

    def pass_on(step, side):
        source = 3 - step if side == 0 else 3 + step
        target = source - 1 if side == 0 else source + 1
        return pltpu.make_async_remote_copy(
            src_ref=window.at[source],
            dst_ref=window.at[target],
            send_sem=s_send.at[side, step],
            recv_sem=s_recv.at[side, step],
            device_id=place(1 if side == 0 else -1),
            device_id_type=MESH,
        )

    pl.semaphore_wait(barrier, 6 + n_col - 1)
    hops = [[pass_on(step, side) for side in range(2)] for step in range(3)]
    hops[0][0].start()
    hops[0][1].start()

    loads[1].wait()
    diags = []
    for i in range(2):
        t = mm(flipped[i], near_v[i, 0])
        turned[i, 3, SK * i : SK * (i + 1), :] = t[RD:, :]
        diags.append(mm(t, basis_v[i]))

    def relay(b):
        for side in range(2):
            hops[b][side].wait_recv()
            hops[b + 1][side].start()

    weights = eliminate(diags, [basis_v[0], basis_v[1]], relay)

    slots, lives = [], []
    for i in range(2):
        spots = []
        for q in range(NB):
            away = nbr_s[i, q] - (2 * me + i) + leaf_total + leaf_total // 2
            spot = lax.rem(away, leaf_total) - leaf_total // 2 + 6
            spots.append(jnp.clip(spot, 0, NB - 1))
        found, alive = [], []
        for o in range(NB):
            slot = jnp.int32(0)
            for q in range(1, NB):
                slot = jnp.where(spots[q] == o, q, slot)
            found.append(slot)
            alive.append(live_s[i, slot].astype(F32))
        slots.append((found, spots))
        lives.append(alive)

    loads[2].wait()

    def turn(e):
        for i in range(2):
            for j in range(2):
                o = 2 * (e - 3) + j - i + 6
                at = pl.ds(SK * j, SK)
                if o == 6:
                    continue
                if 0 <= o < NB:
                    turned[i, e, at, :] = (
                        mm(window[e, at, :], near_v[i, slots[i][0][o]]) * lives[i][o]
                    )
                else:
                    turned[i, e, at, :] = jnp.zeros((SK, M), F32)

    v, vt = [], []
    for i in range(2):
        v.append(weights[i] - 0.5 * basis_v[i, :, RD:])
        vt.append(v[i].T)

    def send(e):
        return pltpu.make_async_remote_copy(
            src_ref=sent.at[e],
            dst_ref=got.at[6 - e],
            send_sem=f_send.at[e],
            recv_sem=f_recv.at[6 - e],
            device_id=place(e - 3),
            device_id_type=MESH,
        )

    def out_and_mine(e):
        sent[e] = jnp.concatenate([mm(turned[i, e], v[i]) for i in range(2)], axis=1)
        for i in range(2):
            ring[e + 4, SK * i : SK * (i + 1), :] = mm(vt[i], turned[i, e], NT)

    sends = {e: send(e) for e in range(7) if e != 3}
    turn(3)
    out_and_mine(3)
    mine = ring[7] + sent[3]
    for i in range(2):
        at = slice(SK * i, SK * (i + 1))
        own_send[at, :] = mine[at, :]
        own_send[at, at] = mm(turned[i, 3, at, :], weights[i])
    ring[7] = own_send[...]
    own_copy = pltpu.make_async_remote_copy(
        src_ref=own_send,
        dst_ref=own_got,
        send_sem=c_sem.at[0],
        recv_sem=c_sem.at[1],
        device_id=partner,
        device_id_type=MESH,
    )
    own_copy.start()
    for e in (2, 4):
        turn(e)
        out_and_mine(e)
        sends[e].start()
    for e in (1, 5):
        turn(e)
        out_and_mine(e)
        sends[e].start()
    for side in range(2):
        hops[2][side].wait_recv()
    for e in (0, 6):
        turn(e)
        out_and_mine(e)
        sends[e].start()

    for e in range(4):
        ring[e] = jnp.zeros((128, 128), F32)
        ring[e + 11] = jnp.zeros((128, 128), F32)
    loads[3].wait()
    loads[4].wait()
    pb_own = pb_v[parent]
    pb_flip = pb_own.T
    own_copy.wait_recv()
    for e in (2, 4):
        sends[6 - e].wait_recv()
        ring[e + 4] += got[e]
    cross = ring[8 - 2 * half]
    here = pl.multiple_of(half * 128, 128)
    there = pl.multiple_of(128 - half * 128, 128)
    joint[pl.ds(here, 128), pl.ds(here, 128)] = own_send[...]
    joint[pl.ds(there, 128), pl.ds(there, 128)] = own_got[...]
    joint[pl.ds(here, 128), pl.ds(there, 128)] = cross
    joint[pl.ds(there, 128), pl.ds(here, 128)] = cross.T
    diag = mm(mm(pb_flip, joint[...]), pb_own)

    mixed_copy = pltpu.make_async_remote_copy(
        src_ref=mixed.at[1 - half],
        dst_ref=mixed_got,
        send_sem=m_sem.at[0],
        recv_sem=m_sem.at[1],
        device_id=partner,
        device_id_type=MESH,
    )

    def mix(b):
        if b != 1:
            return
        for e in (1, 5, 0, 6):
            sends[6 - e].wait_recv()
            ring[e + 4] += got[e]
        for u in range(4):
            skel = pb_v[u, :, RD:]
            mixed[u // 2, :, SK * (u % 2) : SK * (u % 2 + 1)] = mm(
                ring[2 * u + 7 - col], skel[:128]
            ) + mm(ring[2 * u + 8 - col], skel[128:])
        mixed_copy.start()

    (w,) = eliminate([diag], [pb_own], mix)
    parts[...] = jnp.concatenate([w - 0.5 * pb_own[:, RD:], 0.5 * w], axis=1)
    mixed_copy.wait_recv()
    both = mm(parts[pl.ds(here, 128), :], mixed[half], TN) + mm(
        parts[pl.ds(there, 128), :], mixed_got[...], TN
    )
    of = lax.broadcasted_iota(jnp.int32, (SK, 128), 1) // SK + 2 * half
    piece = jnp.where(of == parent, both[SK:], both[:SK])
    share[...] = piece
    spreads = []
    for k in range(1, n_col):
        spreads.append(
            pltpu.make_async_remote_copy(
                src_ref=share,
                dst_ref=shares.at[col],
                send_sem=e_send.at[k - 1],
                recv_sem=e_recv.at[k - 1],
                device_id=(row, lax.rem(col + k, n_col)),
                device_id_type=MESH,
            )
        )
    for spread in spreads:
        spread.start()
    shares[col] = piece

    for e in range(7):
        whole = ring[e + 4]
        for i in range(2):
            for j in range(2):
                o = 2 * (e - 3) + j - i + 6
                if 0 <= o < NB:
                    blocks[i, o] = whole[SK * i : SK * (i + 1), SK * j : SK * (j + 1)]
    for i in range(2):
        for q in range(NB):
            spot = slots[i][1][q] if q else 6
            leaf_o[i, :, SK * q : SK * (q + 1)] = blocks[i, spot]

    gb = gb_v[0]
    gb_flip = gb.T
    for k in range(1, n_col):
        pltpu.make_async_remote_copy(
            src_ref=share,
            dst_ref=shares.at[lax.rem(col - k + n_col, n_col)],
            send_sem=e_send.at[k - 1],
            recv_sem=e_recv.at[k - 1],
            device_id=(row, lax.rem(col + k, n_col)),
            device_id_type=MESH,
        ).wait_recv()
    rows = [jnp.concatenate([shares[2 * p], shares[2 * p + 1]], axis=1) for p in range(4)]
    summed = jnp.concatenate(rows, axis=0)
    summed = summed + summed.T
    for p in range(4):
        par_o[p] = summed[SK * p : SK * (p + 1)]
    t = mm(gb_flip, summed)
    (w,) = eliminate([mm(t, gb)], [gb])
    top_o[0] = mm(t[RD:], w)

    for step in range(3):
        for side in range(2):
            hops[step][side].wait_send()
    for e in sends:
        sends[e].wait_send()
    own_copy.wait_send()
    mixed_copy.wait_send()
    for spread in spreads:
        spread.wait_send()


def on_device(n_leaf, n_col, near, basis, parent_basis, grand_basis, nbr, live, partner):
    hbm = pl.BlockSpec(memory_space=pl.ANY)
    smem = pl.BlockSpec(memory_space=pltpu.SMEM)
    vmem = pl.BlockSpec(memory_space=pltpu.VMEM)
    dma = pltpu.SemaphoreType.DMA
    return pl.pallas_call(
        functools.partial(kernel, n_leaf, n_col),
        out_shape=(
            jax.ShapeDtypeStruct((2, SK, NB * SK), F32),
            jax.ShapeDtypeStruct((4, SK, M), F32),
            jax.ShapeDtypeStruct((1, SK, SK), F32),
        ),
        in_specs=[hbm, hbm, hbm, hbm, smem, smem],
        out_specs=(vmem, vmem, vmem),
        scratch_shapes=[
            pltpu.VMEM((2, NB, M, M), F32),
            pltpu.VMEM((2, M, M), F32),
            pltpu.VMEM((4, M, M), F32),
            pltpu.VMEM((1, M, M), F32),
            pltpu.VMEM((7, 128, M), F32),
            pltpu.VMEM((2, 7, 128, M), F32),
            pltpu.VMEM((8, 128), F32),
            pltpu.VMEM((7, 128, 128), F32),
            pltpu.VMEM((7, 128, 128), F32),
            pltpu.VMEM((128, 128), F32),
            pltpu.VMEM((128, 128), F32),
            pltpu.VMEM((15, 128, 128), F32),
            pltpu.VMEM((M, M), F32),
            pltpu.VMEM((2, 128, 128), F32),
            pltpu.VMEM((128, 128), F32),
            pltpu.VMEM((M, 128), F32),
            pltpu.VMEM((SK, 128), F32),
            pltpu.VMEM((8, SK, 128), F32),
            pltpu.VMEM((2, NB, SK, SK), F32),
            dma((5,)),
            dma((2, 3)),
            dma((2, 3)),
            dma((7,)),
            dma((7,)),
            dma((2,)),
            dma((2,)),
            dma((7,)),
            dma((7,)),
        ],
        compiler_params=pltpu.CompilerParams(
            collective_id=0, has_side_effects=True, vmem_limit_bytes=50 * 1024 * 1024
        ),
    )(near, basis, parent_basis, grand_basis, nbr, live)


def solution(mesh):
    both = ("leaf", "col")
    return jax.shard_map(
        functools.partial(on_device, mesh.shape["leaf"], mesh.shape["col"]),
        mesh=mesh,
        in_specs=(
            P(both, None, None, None),
            P(both, None, None),
            P("leaf", None, None),
            P("leaf", None, None),
            P(both, None),
            P(both, None),
            P(both, None),
        ),
        out_specs=(P(both, None, None), P("leaf", None, None), P("leaf", None, None)),
        check_vma=False,
    )
```

```python
import functools

import jax
import jax.numpy as jnp
from jax import lax
from jax.experimental import pallas as pl
from jax.experimental.pallas import tpu as pltpu
from jax.sharding import PartitionSpec as P

M = 256
SK = 64
RD = 192
NB = 13
G = 16
F32 = jnp.float32
HIGH = lax.Precision.HIGH
MESH = pl.DeviceIdType.MESH
VMEM_ALL = 67_000_000
NN = ((1,), (0,))
NT = ((1,), (1,))
TN = ((0,), (0,))


def mm(a, b, dims=NN):
    return lax.dot_general(a, b, (dims, ((), ())), precision=HIGH, preferred_element_type=F32)


def lane(x, k):
    return jnp.broadcast_to(x[:, k : k + 1], x.shape)


def sublane(x, k):
    return jnp.broadcast_to(x[k : k + 1, :], x.shape)


def tree_sum(terms):
    while len(terms) > 1:
        terms = [
            terms[i] + terms[i + 1] if i + 1 < len(terms) else terms[i]
            for i in range(0, len(terms), 2)
        ]
    return terms[0]


def forward_steps(rows_all, size, found):
    depth = G // 8
    row_ids = lax.broadcasted_iota(jnp.int32, (8, 128), 0)
    before, after = [], []
    for g in range(size // G):
        top, k0 = depth * g, G * g
        rows = list(rows_all[top : top + depth])
        before += rows
        following = range(top + depth, min(top + 2 * depth, size // 8))
        later = range(top + 2 * depth, size // 8)
        ahead = {u: [lane(rows_all[u], k0 + j) for j in range(G)] for u in following}
        cols = [[lane(rows[h], k0 + j) for h in range(depth)] for j in range(G)]
        scale = [None] * depth
        for k in range(G):
            kh, ks = divmod(k, 8)
            inverse = 1.0 / sublane(cols[k][kh], ks)
            here = row_ids == ks
            scale[kh] = inverse if ks == 0 else jnp.where(here, inverse, scale[kh])
            factor = [c * inverse for c in cols[k]]
            factor[kh] = jnp.where(here, 0.0, factor[kh])
            for j in range(k + 1, G):
                pivot = sublane(cols[j][kh], ks)
                cols[j] = [cols[j][h] - factor[h] * pivot for h in range(depth)]
            pivot = sublane(rows[kh], ks)
            rows = [rows[h] - factor[h] * pivot for h in range(depth)]
            yield
        rows = [rows[h] * scale[h] for h in range(depth)]
        after += rows
        for u in following:
            rows_all[u] = rows_all[u] - tree_sum(
                [ahead[u][j] * sublane(rows[j // 8], j % 8) for j in range(G)]
            )
        if later:
            left = jnp.concatenate([rows_all[u] for u in later], axis=0)[:, k0 : k0 + G]
            change = mm(left, jnp.concatenate(rows, axis=0))
            for n, u in enumerate(later):
                rows_all[u] = rows_all[u] - change[8 * n : 8 * n + 8]
    found.append((before, after))


def half_inverses(blocks):
    size = blocks[0].shape[0]
    r = lax.broadcasted_iota(jnp.int32, (size, size), 0)
    c = lax.broadcasted_iota(jnp.int32, (size, size), 1)
    eye = jnp.where(r == c, 1.0, 0.0).astype(F32)
    found, steps = [], []
    for block in blocks:
        wide = jnp.concatenate([block, eye], axis=1)
        mine = []
        found.append(mine)
        steps.append(
            forward_steps([wide[8 * i : 8 * i + 8] for i in range(size // 8)], size, mine)
        )
    going = True
    while going:
        for step in steps:
            if next(step, 0) == 0:
                going = False
    out = []
    for mine in found:
        before, after = mine[0]
        out.append(
            (
                jnp.concatenate(before, axis=0)[:, size:],
                jnp.concatenate(after, axis=0)[:, size:],
            )
        )
    return out


def eliminate(diags, bases, between=None):
    upper = [d[:RD] for d in diags]
    lower = list(bases)
    for b in range(3):
        halves = half_inverses([a[:SK, :SK] for a in upper])
        for i, (before, after) in enumerate(halves):
            a, e = upper[i], lower[i]
            z = mm(after, a[:SK, SK:])
            if b < 2:
                upper[i] = a[SK:, SK:] - mm(mm(a[SK:, :SK], before, NT), z)
            lower[i] = e[:, SK:] - mm(mm(e[:, :SK], before, NT), z)
        if between is not None and b < 2:
            between(b)
    return lower


def kernel(
    n_leaf,
    n_col,
    near_h,
    basis_h,
    pb_h,
    nbr_h,
    live_h,
    ring_o,
    joined_o,
    near_v,
    basis_v,
    pb_v,
    window,
    turned,
    sent,
    got,
    own_send,
    own_got,
    ring,
    joint,
    mixed,
    mixed_got,
    parts,
    share,
    shares,
    joined,
    nbr_s,
    live_s,
    load_sem,
    s_send,
    s_recv,
    f_send,
    f_recv,
    c_sem,
    m_sem,
    e_send,
    e_recv,
    save_sem,
):
    total = n_leaf * n_col
    leaf_total = 2 * total
    row = lax.axis_index("leaf")
    col = lax.axis_index("col")
    me = row * n_col + col
    half = lax.rem(col, 2)
    parent = col // 2

    def place(k):
        n = lax.rem(me + k + total, total)
        return (n // n_col, lax.rem(n, n_col))

    partner = (row, col + 1 - 2 * half)

    loads = [
        pltpu.make_async_copy(nbr_h, nbr_s, load_sem.at[4]),
        pltpu.make_async_copy(live_h, live_s, load_sem.at[5]),
        pltpu.make_async_copy(basis_h, basis_v, load_sem.at[0]),
        pltpu.make_async_copy(near_h.at[:, 0], near_v.at[:, 0], load_sem.at[1]),
        pltpu.make_async_copy(near_h.at[:, 1:], near_v.at[:, 1:], load_sem.at[2]),
        pltpu.make_async_copy(pb_h, pb_v, load_sem.at[3]),
    ]
    for load in loads:
        load.start()
    barrier = pltpu.get_barrier_semaphore()
    for k in (1, -1, 2, -2, 3, -3):
        pl.semaphore_signal(barrier, inc=1, device_id=place(k), device_id_type=MESH)
    for k in range(1, n_col):
        pl.semaphore_signal(
            barrier, inc=1, device_id=(row, lax.rem(col + k, n_col)), device_id_type=MESH
        )

    loads[2].wait()
    flipped = []
    for i in range(2):
        t = basis_v[i].T
        flipped.append(t)
        window[3, SK * i : SK * (i + 1), :] = t[RD:, :]

    def pass_on(step, side):
        source = 3 - step if side == 0 else 3 + step
        target = source - 1 if side == 0 else source + 1
        return pltpu.make_async_remote_copy(
            src_ref=window.at[source],
            dst_ref=window.at[target],
            send_sem=s_send.at[side, step],
            recv_sem=s_recv.at[side, step],
            device_id=place(1 if side == 0 else -1),
            device_id_type=MESH,
        )

    pl.semaphore_wait(barrier, 6 + n_col - 1)
    hops = [[pass_on(step, side) for side in range(2)] for step in range(3)]
    hops[0][0].start()
    hops[0][1].start()

    loads[3].wait()
    diags = []
    for i in range(2):
        t = mm(flipped[i], near_v[i, 0])
        turned[i, 3, SK * i : SK * (i + 1), :] = t[RD:, :]
        diags.append(mm(t, basis_v[i]))

    loads[0].wait()
    loads[1].wait()
    slots, lives = [], []
    for i in range(2):
        spots = []
        for q in range(NB):
            away = nbr_s[i, q] - (2 * me + i) + leaf_total + leaf_total // 2
            spot = lax.rem(away, leaf_total) - leaf_total // 2 + 6
            spots.append(jnp.clip(spot, 0, NB - 1))
        found, alive = [], []
        for o in range(NB):
            slot = jnp.int32(0)
            for q in range(1, NB):
                slot = jnp.where(spots[q] == o, q, slot)
            found.append(slot)
            alive.append(live_s[i, slot].astype(F32))
        slots.append((found, spots))
        lives.append(alive)

    loads[4].wait()

    def turn(e):
        for i in range(2):
            for j in range(2):
                o = 2 * (e - 3) + j - i + 6
                at = pl.ds(SK * j, SK)
                if o == 6:
                    continue
                if 0 <= o < NB:
                    turned[i, e, at, :] = (
                        mm(window[e, at, :], near_v[i, slots[i][0][o]]) * lives[i][o]
                    )
                else:
                    turned[i, e, at, :] = jnp.zeros((SK, M), F32)

    def relay(b):
        for side in range(2):
            hops[b][side].wait_recv()
            hops[b + 1][side].start()

    def early(b):
        if b == 1:
            relay(0)
            turn(3)
            turn(2)
            turn(4)

    weights = eliminate(diags, [basis_v[0], basis_v[1]], early)

    v, vt = [], []
    for i in range(2):
        v.append(weights[i] - 0.5 * basis_v[i, :, RD:])
        vt.append(v[i].T)

    def send(e):
        return pltpu.make_async_remote_copy(
            src_ref=sent.at[e],
            dst_ref=got.at[6 - e],
            send_sem=f_send.at[e],
            recv_sem=f_recv.at[6 - e],
            device_id=place(e - 3),
            device_id_type=MESH,
        )

    def out_and_mine(e):
        sent[e] = jnp.concatenate([mm(turned[i, e], v[i]) for i in range(2)], axis=1)
        for i in range(2):
            ring[e + 4, SK * i : SK * (i + 1), :] = mm(vt[i], turned[i, e], NT)

    sends = {e: send(e) for e in range(7) if e != 3}
    out_and_mine(3)
    mine = ring[7] + sent[3]
    for i in range(2):
        at = slice(SK * i, SK * (i + 1))
        own_send[at, :] = mine[at, :]
        own_send[at, at] = mm(turned[i, 3, at, :], weights[i])
    ring[7] = own_send[...]
    own_copy = pltpu.make_async_remote_copy(
        src_ref=own_send,
        dst_ref=own_got,
        send_sem=c_sem.at[0],
        recv_sem=c_sem.at[1],
        device_id=partner,
        device_id_type=MESH,
    )
    own_copy.start()
    for e in (2, 4):
        out_and_mine(e)
        sends[e].start()
    relay(1)
    for e in (1, 5):
        turn(e)
        out_and_mine(e)
        sends[e].start()
    for side in range(2):
        hops[2][side].wait_recv()
    for e in (0, 6):
        turn(e)
        out_and_mine(e)
        sends[e].start()

    for e in range(4):
        ring[e] = jnp.zeros((128, 128), F32)
        ring[e + 11] = jnp.zeros((128, 128), F32)
    loads[5].wait()
    pb_own = pb_v[parent]
    pb_flip = pb_own.T
    own_copy.wait_recv()
    for e in (2, 4):
        sends[6 - e].wait_recv()
        ring[e + 4] += got[e]
    cross = ring[8 - 2 * half]
    here = pl.multiple_of(half * 128, 128)
    there = pl.multiple_of(128 - half * 128, 128)
    joint[pl.ds(here, 128), pl.ds(here, 128)] = own_send[...]
    joint[pl.ds(there, 128), pl.ds(there, 128)] = own_got[...]
    joint[pl.ds(here, 128), pl.ds(there, 128)] = cross
    joint[pl.ds(there, 128), pl.ds(here, 128)] = cross.T
    diag = mm(mm(pb_flip, joint[...]), pb_own)

    mixed_copy = pltpu.make_async_remote_copy(
        src_ref=mixed.at[1 - half],
        dst_ref=mixed_got,
        send_sem=m_sem.at[0],
        recv_sem=m_sem.at[1],
        device_id=partner,
        device_id_type=MESH,
    )

    def mix(b):
        if b != 1:
            return
        for e in (1, 5, 0, 6):
            sends[6 - e].wait_recv()
            ring[e + 4] += got[e]
        for u in range(4):
            skel = pb_v[u, :, RD:]
            mixed[u // 2, :, SK * (u % 2) : SK * (u % 2 + 1)] = mm(
                ring[2 * u + 7 - col], skel[:128]
            ) + mm(ring[2 * u + 8 - col], skel[128:])
        mixed_copy.start()

    (w,) = eliminate([diag], [pb_own], mix)
    parts[...] = jnp.concatenate([w - 0.5 * pb_own[:, RD:], 0.5 * w], axis=1)
    mixed_copy.wait_recv()
    both = mm(parts[pl.ds(here, 128), :], mixed[half], TN) + mm(
        parts[pl.ds(there, 128), :], mixed_got[...], TN
    )
    of = lax.broadcasted_iota(jnp.int32, (SK, 128), 1) // SK + 2 * half
    piece = jnp.where(of == parent, both[SK:], both[:SK])
    share[...] = piece
    spreads = []
    for k in range(1, n_col):
        spreads.append(
            pltpu.make_async_remote_copy(
                src_ref=share,
                dst_ref=shares.at[col],
                send_sem=e_send.at[k - 1],
                recv_sem=e_recv.at[k - 1],
                device_id=(row, lax.rem(col + k, n_col)),
                device_id_type=MESH,
            )
        )
    for k in (4, 3, 5, 2, 6, 1, 7):
        spreads[k - 1].start()
    shares[col] = piece
    ring_save = pltpu.make_async_copy(ring.at[4:11], ring_o, save_sem.at[0])
    ring_save.start()

    for k in range(1, n_col):
        pltpu.make_async_remote_copy(
            src_ref=share,
            dst_ref=shares.at[lax.rem(col - k + n_col, n_col)],
            send_sem=e_send.at[k - 1],
            recv_sem=e_recv.at[k - 1],
            device_id=(row, lax.rem(col + k, n_col)),
            device_id_type=MESH,
        ).wait_recv()
    rows = [jnp.concatenate([shares[2 * p], shares[2 * p + 1]], axis=1) for p in range(4)]
    summed = jnp.concatenate(rows, axis=0)
    joined[...] = summed + summed.T
    joined_save = pltpu.make_async_copy(joined, joined_o, save_sem.at[1])
    joined_save.start()

    for step in range(3):
        for side in range(2):
            hops[step][side].wait_send()
    for e in sends:
        sends[e].wait_send()
    own_copy.wait_send()
    mixed_copy.wait_send()
    for spread in spreads:
        spread.wait_send()
    ring_save.wait()
    joined_save.wait()


def finish(
    n_leaf,
    n_col,
    ring_h,
    joined_h,
    gb_h,
    nbr_h,
    leaf_o,
    par_o,
    top_o,
    ring,
    joined,
    gb_v,
    nbr_s,
    blocks,
    leaf_v,
    load_sem,
    leaf_sem,
    par_sem,
):
    leaf_total = 2 * n_leaf * n_col
    me = lax.axis_index("leaf") * n_col + lax.axis_index("col")
    loads = [
        pltpu.make_async_copy(gb_h, gb_v, load_sem.at[0]),
        pltpu.make_async_copy(joined_h, joined, load_sem.at[1]),
        pltpu.make_async_copy(nbr_h, nbr_s, load_sem.at[2]),
        pltpu.make_async_copy(ring_h, ring, load_sem.at[3]),
    ]
    for load in loads:
        load.start()
    for load in loads:
        load.wait()
    saves = [
        pltpu.make_async_copy(joined.at[pl.ds(SK * p, SK)], par_o.at[p], par_sem.at[p])
        for p in range(4)
    ]
    for save in saves:
        save.start()
    for e in range(7):
        whole = ring[e]
        for i in range(2):
            for j in range(2):
                o = 2 * (e - 3) + j - i + 6
                if 0 <= o < NB:
                    blocks[i, o] = whole[SK * i : SK * (i + 1), SK * j : SK * (j + 1)]
    for i in range(2):
        for q in range(NB):
            away = nbr_s[i, q] - (2 * me + i) + leaf_total + leaf_total // 2
            spot = lax.rem(away, leaf_total) - leaf_total // 2 + 6
            leaf_v[i, :, SK * q : SK * (q + 1)] = blocks[i, jnp.clip(spot, 0, NB - 1)]
    saves.append(pltpu.make_async_copy(leaf_v, leaf_o, leaf_sem))
    saves[-1].start()
    gb = gb_v[0]
    t = mm(gb.T, joined[...])
    (w,) = eliminate([mm(t, gb)], [gb])
    top_o[0] = mm(t[RD:], w)
    for save in saves:
        save.wait()


def on_device(n_leaf, n_col, near, basis, parent_basis, grand_basis, nbr, live, partner):
    hbm = pl.BlockSpec(memory_space=pltpu.HBM)
    vmem = pl.BlockSpec(memory_space=pltpu.VMEM)
    dma = pltpu.SemaphoreType.DMA
    ring, joined = pl.pallas_call(
        functools.partial(kernel, n_leaf, n_col),
        out_shape=(
            jax.ShapeDtypeStruct((7, 128, 128), F32),
            jax.ShapeDtypeStruct((M, M), F32),
        ),
        in_specs=[hbm] * 5,
        out_specs=(hbm, hbm),
        scratch_shapes=[
            pltpu.VMEM((2, NB, M, M), F32),
            pltpu.VMEM((2, M, M), F32),
            pltpu.VMEM((4, M, M), F32),
            pltpu.VMEM((7, 128, M), F32),
            pltpu.VMEM((2, 7, 128, M), F32),
            pltpu.VMEM((7, 128, 128), F32),
            pltpu.VMEM((7, 128, 128), F32),
            pltpu.VMEM((128, 128), F32),
            pltpu.VMEM((128, 128), F32),
            pltpu.VMEM((15, 128, 128), F32),
            pltpu.VMEM((M, M), F32),
            pltpu.VMEM((2, 128, 128), F32),
            pltpu.VMEM((128, 128), F32),
            pltpu.VMEM((M, 128), F32),
            pltpu.VMEM((SK, 128), F32),
            pltpu.VMEM((8, SK, 128), F32),
            pltpu.VMEM((M, M), F32),
            pltpu.SMEM((2, NB), jnp.int32),
            pltpu.SMEM((2, NB), jnp.int32),
            dma((6,)),
            dma((2, 3)),
            dma((2, 3)),
            dma((7,)),
            dma((7,)),
            dma((2,)),
            dma((2,)),
            dma((7,)),
            dma((7,)),
            dma((2,)),
        ],
        compiler_params=pltpu.CompilerParams(
            collective_id=0, has_side_effects=True, vmem_limit_bytes=VMEM_ALL
        ),
    )(near, basis, parent_basis, nbr, live)
    return pl.pallas_call(
        functools.partial(finish, n_leaf, n_col),
        out_shape=(
            jax.ShapeDtypeStruct((2, SK, NB * SK), F32),
            jax.ShapeDtypeStruct((4, SK, M), F32),
            jax.ShapeDtypeStruct((1, SK, SK), F32),
        ),
        in_specs=[hbm] * 4,
        out_specs=(hbm, hbm, vmem),
        scratch_shapes=[
            pltpu.VMEM((7, 128, 128), F32),
            pltpu.VMEM((M, M), F32),
            pltpu.VMEM((1, M, M), F32),
            pltpu.SMEM((2, NB), jnp.int32),
            pltpu.VMEM((2, NB, SK, SK), F32),
            pltpu.VMEM((2, SK, NB * SK), F32),
            dma((4,)),
            dma(()),
            dma((4,)),
        ],
        compiler_params=pltpu.CompilerParams(vmem_limit_bytes=VMEM_ALL),
    )(ring, joined, grand_basis, nbr)


def solution(mesh):
    both = ("leaf", "col")
    return jax.shard_map(
        functools.partial(on_device, mesh.shape["leaf"], mesh.shape["col"]),
        mesh=mesh,
        in_specs=(
            P(both, None, None, None),
            P(both, None, None),
            P("leaf", None, None),
            P("leaf", None, None),
            P(both, None),
            P(both, None),
            P(both, None),
        ),
        out_specs=(P(both, None, None), P("leaf", None, None), P("leaf", None, None)),
        check_vma=False,
    )
```

```python
import functools

import jax
import jax.numpy as jnp
from jax import lax
from jax.experimental import pallas as pl
from jax.experimental.pallas import tpu as pltpu
from jax.sharding import PartitionSpec as P

M = 256
SK = 64
RD = 192
NB = 13
G = 16
F32 = jnp.float32
HIGH = lax.Precision.HIGH
MESH = pl.DeviceIdType.MESH
VMEM_ALL = 67_000_000
NN = ((1,), (0,))
NT = ((1,), (1,))
TN = ((0,), (0,))


def mm(a, b, dims=NN):
    return lax.dot_general(a, b, (dims, ((), ())), precision=HIGH, preferred_element_type=F32)


def lane(x, k):
    return jnp.broadcast_to(x[:, k : k + 1], x.shape)


def sublane(x, k):
    return jnp.broadcast_to(x[k : k + 1, :], x.shape)


def tree_sum(terms):
    while len(terms) > 1:
        terms = [
            terms[i] + terms[i + 1] if i + 1 < len(terms) else terms[i]
            for i in range(0, len(terms), 2)
        ]
    return terms[0]


def forward_steps(rows_all, size, found):
    depth = G // 8
    row_ids = lax.broadcasted_iota(jnp.int32, (8, 128), 0)
    before, after = [], []
    for g in range(size // G):
        top, k0 = depth * g, G * g
        rows = list(rows_all[top : top + depth])
        before += rows
        following = range(top + depth, min(top + 2 * depth, size // 8))
        later = range(top + 2 * depth, size // 8)
        ahead = {u: [lane(rows_all[u], k0 + j) for j in range(G)] for u in following}
        cols = [[lane(rows[h], k0 + j) for h in range(depth)] for j in range(G)]
        scale = [None] * depth
        for k in range(G):
            kh, ks = divmod(k, 8)
            inverse = 1.0 / sublane(cols[k][kh], ks)
            here = row_ids == ks
            scale[kh] = inverse if ks == 0 else jnp.where(here, inverse, scale[kh])
            factor = [c * inverse for c in cols[k]]
            factor[kh] = jnp.where(here, 0.0, factor[kh])
            for j in range(k + 1, G):
                pivot = sublane(cols[j][kh], ks)
                cols[j] = [cols[j][h] - factor[h] * pivot for h in range(depth)]
            pivot = sublane(rows[kh], ks)
            rows = [rows[h] - factor[h] * pivot for h in range(depth)]
            yield
        rows = [rows[h] * scale[h] for h in range(depth)]
        after += rows
        for u in following:
            rows_all[u] = rows_all[u] - tree_sum(
                [ahead[u][j] * sublane(rows[j // 8], j % 8) for j in range(G)]
            )
        if later:
            left = jnp.concatenate([rows_all[u] for u in later], axis=0)[:, k0 : k0 + G]
            change = mm(left, jnp.concatenate(rows, axis=0))
            for n, u in enumerate(later):
                rows_all[u] = rows_all[u] - change[8 * n : 8 * n + 8]
    found.append((before, after))


def half_inverses(blocks):
    size = blocks[0].shape[0]
    r = lax.broadcasted_iota(jnp.int32, (size, size), 0)
    c = lax.broadcasted_iota(jnp.int32, (size, size), 1)
    eye = jnp.where(r == c, 1.0, 0.0).astype(F32)
    found, steps = [], []
    for block in blocks:
        wide = jnp.concatenate([block, eye], axis=1)
        mine = []
        found.append(mine)
        steps.append(
            forward_steps([wide[8 * i : 8 * i + 8] for i in range(size // 8)], size, mine)
        )
    going = True
    while going:
        for step in steps:
            if next(step, 0) == 0:
                going = False
    out = []
    for mine in found:
        before, after = mine[0]
        out.append(
            (
                jnp.concatenate(before, axis=0)[:, size:],
                jnp.concatenate(after, axis=0)[:, size:],
            )
        )
    return out


def eliminate(diags, bases, between=None):
    upper = [d[:RD] for d in diags]
    lower = list(bases)
    for b in range(3):
        halves = half_inverses([a[:SK, :SK] for a in upper])
        for i, (before, after) in enumerate(halves):
            a, e = upper[i], lower[i]
            z = mm(after, a[:SK, SK:])
            if b < 2:
                upper[i] = a[SK:, SK:] - mm(mm(a[SK:, :SK], before, NT), z)
            lower[i] = e[:, SK:] - mm(mm(e[:, :SK], before, NT), z)
        if between is not None and b < 2:
            between(b)
    return lower


def kernel(
    n_leaf,
    n_col,
    near_h,
    basis_h,
    pb_h,
    nbr_h,
    live_h,
    ring_o,
    joined_o,
    near_v,
    basis_v,
    pb_v,
    window,
    turned,
    sent,
    got,
    own_send,
    own_got,
    ring,
    joint,
    mixed,
    mixed_got,
    parts,
    share,
    shares,
    joined,
    nbr_s,
    live_s,
    load_sem,
    s_send,
    s_recv,
    f_send,
    f_recv,
    c_sem,
    m_sem,
    e_send,
    e_recv,
    r_sem,
    save_sem,
):
    total = n_leaf * n_col
    leaf_total = 2 * total
    row = lax.axis_index("leaf")
    col = lax.axis_index("col")
    me = row * n_col + col
    half = lax.rem(col, 2)
    parent = col // 2

    def place(k):
        n = lax.rem(me + k + total, total)
        return (n // n_col, lax.rem(n, n_col))

    partner = (row, col + 1 - 2 * half)

    loads = [
        pltpu.make_async_copy(nbr_h, nbr_s, load_sem.at[4]),
        pltpu.make_async_copy(live_h, live_s, load_sem.at[5]),
        pltpu.make_async_copy(basis_h, basis_v, load_sem.at[0]),
        pltpu.make_async_copy(near_h.at[:, 0], near_v.at[:, 0], load_sem.at[1]),
        pltpu.make_async_copy(near_h.at[:, 1:], near_v.at[:, 1:], load_sem.at[2]),
        pltpu.make_async_copy(pb_h, pb_v, load_sem.at[3]),
    ]
    for load in loads:
        load.start()
    barrier = pltpu.get_barrier_semaphore()
    for k in (1, -1, 2, -2, 3, -3):
        pl.semaphore_signal(barrier, inc=1, device_id=place(k), device_id_type=MESH)
    for k in range(1, n_col):
        pl.semaphore_signal(
            barrier, inc=1, device_id=(row, lax.rem(col + k, n_col)), device_id_type=MESH
        )

    loads[2].wait()
    for i in range(2):
        window[3, SK * i : SK * (i + 1), :] = basis_v[i, :, RD:].T

    def pass_on(step, side, j):
        source = 3 - step if side == 0 else 3 + step
        target = source - 1 if side == 0 else source + 1
        return pltpu.make_async_remote_copy(
            src_ref=window.at[source, pl.ds(SK * j, SK)],
            dst_ref=window.at[target, pl.ds(SK * j, SK)],
            send_sem=s_send.at[side, step, j],
            recv_sem=s_recv.at[side, step, j],
            device_id=place(1 if side == 0 else -1),
            device_id_type=MESH,
        )

    pl.semaphore_wait(barrier, 6 + n_col - 1)
    hops = [
        [pass_on(step, side, j) for j in range(2) for side in range(2)] for step in range(3)
    ]
    for hop in hops[0]:
        hop.start()
    flipped = [basis_v[i].T for i in range(2)]

    loads[3].wait()
    diags = []
    for i in range(2):
        t = mm(flipped[i], near_v[i, 0])
        turned[i, 3, SK * i : SK * (i + 1), :] = t[RD:, :]
        diags.append(mm(t, basis_v[i]))

    loads[0].wait()
    loads[1].wait()
    slots, lives = [], []
    for i in range(2):
        spots = []
        for q in range(NB):
            away = nbr_s[i, q] - (2 * me + i) + leaf_total + leaf_total // 2
            spot = lax.rem(away, leaf_total) - leaf_total // 2 + 6
            spots.append(jnp.clip(spot, 0, NB - 1))
        found, alive = [], []
        for o in range(NB):
            slot = jnp.int32(0)
            for q in range(1, NB):
                slot = jnp.where(spots[q] == o, q, slot)
            found.append(slot)
            alive.append(live_s[i, slot].astype(F32))
        slots.append((found, spots))
        lives.append(alive)

    loads[4].wait()

    def turn(e):
        for i in range(2):
            for j in range(2):
                o = 2 * (e - 3) + j - i + 6
                at = pl.ds(SK * j, SK)
                if o == 6:
                    continue
                if 0 <= o < NB:
                    turned[i, e, at, :] = (
                        mm(window[e, at, :], near_v[i, slots[i][0][o]]) * lives[i][o]
                    )
                else:
                    turned[i, e, at, :] = jnp.zeros((SK, M), F32)

    def relay(b):
        for hop, onward in zip(hops[b], hops[b + 1]):
            hop.wait_recv()
            onward.start()

    def early(b):
        if b == 1:
            relay(0)
            turn(3)
            turn(2)
            turn(4)

    weights = eliminate(diags, [basis_v[0], basis_v[1]], early)
    relay(1)

    v, vt = [], []
    for i in range(2):
        v.append(weights[i] - 0.5 * basis_v[i, :, RD:])
        vt.append(v[i].T)

    def send(e):
        return pltpu.make_async_remote_copy(
            src_ref=sent.at[e],
            dst_ref=got.at[6 - e],
            send_sem=f_send.at[e],
            recv_sem=f_recv.at[6 - e],
            device_id=place(e - 3),
            device_id_type=MESH,
        )

    def out_and_mine(e):
        sent[e] = jnp.concatenate([mm(turned[i, e], v[i]) for i in range(2)], axis=1)
        for i in range(2):
            ring[e + 4, SK * i : SK * (i + 1), :] = mm(vt[i], turned[i, e], NT)

    sends = {e: send(e) for e in range(7) if e != 3}
    out_and_mine(3)
    mine = ring[7] + sent[3]
    for i in range(2):
        at = slice(SK * i, SK * (i + 1))
        own_send[at, :] = mine[at, :]
        own_send[at, at] = mm(turned[i, 3, at, :], weights[i])
    ring[7] = own_send[...]
    own_copy = pltpu.make_async_remote_copy(
        src_ref=own_send,
        dst_ref=own_got,
        send_sem=c_sem.at[0],
        recv_sem=c_sem.at[1],
        device_id=partner,
        device_id_type=MESH,
    )
    own_copy.start()
    for e in (2, 4):
        out_and_mine(e)
        sends[e].start()
    for e in (1, 5):
        turn(e)
        out_and_mine(e)
        sends[e].start()
    for hop in hops[2]:
        hop.wait_recv()
    for e in (0, 6):
        turn(e)
        out_and_mine(e)
        sends[e].start()

    for e in range(4):
        ring[e] = jnp.zeros((128, 128), F32)
        ring[e + 11] = jnp.zeros((128, 128), F32)
    loads[5].wait()
    pb_own = pb_v[parent]
    pb_flip = pb_own.T
    own_copy.wait_recv()
    for e in (2, 4):
        sends[6 - e].wait_recv()
        ring[e + 4] += got[e]
    cross = ring[8 - 2 * half]
    here = pl.multiple_of(half * 128, 128)
    there = pl.multiple_of(128 - half * 128, 128)
    joint[pl.ds(here, 128), pl.ds(here, 128)] = own_send[...]
    joint[pl.ds(there, 128), pl.ds(there, 128)] = own_got[...]
    joint[pl.ds(here, 128), pl.ds(there, 128)] = cross
    joint[pl.ds(there, 128), pl.ds(here, 128)] = cross.T
    diag = mm(mm(pb_flip, joint[...]), pb_own)

    mixed_copy = pltpu.make_async_remote_copy(
        src_ref=mixed.at[1 - half],
        dst_ref=mixed_got,
        send_sem=m_sem.at[0],
        recv_sem=m_sem.at[1],
        device_id=partner,
        device_id_type=MESH,
    )

    def mix(b):
        if b != 1:
            return
        for e in (1, 5, 0, 6):
            sends[6 - e].wait_recv()
            ring[e + 4] += got[e]
        for u in range(4):
            skel = pb_v[u, :, RD:]
            mixed[u // 2, :, SK * (u % 2) : SK * (u % 2 + 1)] = mm(
                ring[2 * u + 7 - col], skel[:128]
            ) + mm(ring[2 * u + 8 - col], skel[128:])
        mixed_copy.start()

    (w,) = eliminate([diag], [pb_own], mix)
    parts[...] = jnp.concatenate([w - 0.5 * pb_own[:, RD:], 0.5 * w], axis=1)
    mixed_copy.wait_recv()
    both = mm(parts[pl.ds(here, 128), :], mixed[half], TN) + mm(
        parts[pl.ds(there, 128), :], mixed_got[...], TN
    )
    of = lax.broadcasted_iota(jnp.int32, (SK, 128), 1) // SK + 2 * half
    piece = jnp.where(of == parent, both[SK:], both[:SK])
    share[...] = piece
    spreads = {}
    for k in (3, 5, 2, 6, 1, 7):
        spreads[k] = pltpu.make_async_remote_copy(
            src_ref=share,
            dst_ref=shares.at[col],
            send_sem=e_send.at[k - 1],
            recv_sem=e_recv.at[k - 1],
            device_id=(row, lax.rem(col + k, n_col)),
            device_id_type=MESH,
        )
        spreads[k].start()
    shares[col] = piece
    ring_save = pltpu.make_async_copy(ring.at[4:11], ring_o, save_sem.at[0])
    ring_save.start()

    onwards = []
    for k, step, side in ((3, 1, 0), (5, n_col - 1, 1)):
        spreads[k].wait_recv()
        source = lax.rem(col - k + n_col, n_col)
        onward = pltpu.make_async_remote_copy(
            src_ref=shares.at[source, pl.ds(32 * side, 32)],
            dst_ref=shares.at[source, pl.ds(32 * side, 32)],
            send_sem=r_sem.at[side],
            recv_sem=r_sem.at[2 + side],
            device_id=(row, lax.rem(col + step, n_col)),
            device_id_type=MESH,
        )
        onward.start()
        onwards.append(onward)
    for k in (2, 6, 1, 7):
        spreads[k].wait_recv()
    for onward in onwards:
        onward.wait_recv()
    rows = [jnp.concatenate([shares[2 * p], shares[2 * p + 1]], axis=1) for p in range(4)]
    summed = jnp.concatenate(rows, axis=0)
    joined[...] = summed + summed.T
    joined_save = pltpu.make_async_copy(joined, joined_o, save_sem.at[1])
    joined_save.start()

    for step in range(3):
        for hop in hops[step]:
            hop.wait_send()
    for e in sends:
        sends[e].wait_send()
    own_copy.wait_send()
    mixed_copy.wait_send()
    for k in spreads:
        spreads[k].wait_send()
    for onward in onwards:
        onward.wait_send()
    ring_save.wait()
    joined_save.wait()


def finish(
    n_leaf,
    n_col,
    ring_h,
    joined_h,
    gb_h,
    nbr_h,
    leaf_o,
    par_o,
    top_o,
    ring,
    joined,
    gb_v,
    nbr_s,
    blocks,
    leaf_v,
    load_sem,
    leaf_sem,
    par_sem,
):
    leaf_total = 2 * n_leaf * n_col
    me = lax.axis_index("leaf") * n_col + lax.axis_index("col")
    loads = [
        pltpu.make_async_copy(gb_h, gb_v, load_sem.at[0]),
        pltpu.make_async_copy(joined_h, joined, load_sem.at[1]),
        pltpu.make_async_copy(nbr_h, nbr_s, load_sem.at[2]),
        pltpu.make_async_copy(ring_h, ring, load_sem.at[3]),
    ]
    for load in loads:
        load.start()
    loads[0].wait()
    loads[1].wait()
    saves = [
        pltpu.make_async_copy(joined.at[pl.ds(SK * p, SK)], par_o.at[p], par_sem.at[p])
        for p in range(4)
    ]
    for save in saves:
        save.start()
    def tidy(b):
        if b:
            return
        loads[2].wait()
        loads[3].wait()
        for e in range(7):
            whole = ring[e]
            for i in range(2):
                for j in range(2):
                    o = 2 * (e - 3) + j - i + 6
                    if 0 <= o < NB:
                        blocks[i, o] = whole[SK * i : SK * (i + 1), SK * j : SK * (j + 1)]
        for i in range(2):
            for q in range(NB):
                away = nbr_s[i, q] - (2 * me + i) + leaf_total + leaf_total // 2
                spot = lax.rem(away, leaf_total) - leaf_total // 2 + 6
                leaf_v[i, :, SK * q : SK * (q + 1)] = blocks[i, jnp.clip(spot, 0, NB - 1)]
        saves.append(pltpu.make_async_copy(leaf_v, leaf_o, leaf_sem))
        saves[-1].start()

    gb = gb_v[0]
    t = mm(gb.T, joined[...])
    (w,) = eliminate([mm(t, gb)], [gb], tidy)
    top_o[0] = mm(t[RD:], w)
    for save in saves:
        save.wait()


def on_device(n_leaf, n_col, near, basis, parent_basis, grand_basis, nbr, live, partner):
    hbm = pl.BlockSpec(memory_space=pltpu.HBM)
    vmem = pl.BlockSpec(memory_space=pltpu.VMEM)
    dma = pltpu.SemaphoreType.DMA
    ring, joined = pl.pallas_call(
        functools.partial(kernel, n_leaf, n_col),
        out_shape=(
            jax.ShapeDtypeStruct((7, 128, 128), F32),
            jax.ShapeDtypeStruct((M, M), F32),
        ),
        in_specs=[hbm] * 5,
        out_specs=(hbm, hbm),
        scratch_shapes=[
            pltpu.VMEM((2, NB, M, M), F32),
            pltpu.VMEM((2, M, M), F32),
            pltpu.VMEM((4, M, M), F32),
            pltpu.VMEM((7, 128, M), F32),
            pltpu.VMEM((2, 7, 128, M), F32),
            pltpu.VMEM((7, 128, 128), F32),
            pltpu.VMEM((7, 128, 128), F32),
            pltpu.VMEM((128, 128), F32),
            pltpu.VMEM((128, 128), F32),
            pltpu.VMEM((15, 128, 128), F32),
            pltpu.VMEM((M, M), F32),
            pltpu.VMEM((2, 128, 128), F32),
            pltpu.VMEM((128, 128), F32),
            pltpu.VMEM((M, 128), F32),
            pltpu.VMEM((SK, 128), F32),
            pltpu.VMEM((8, SK, 128), F32),
            pltpu.VMEM((M, M), F32),
            pltpu.SMEM((2, NB), jnp.int32),
            pltpu.SMEM((2, NB), jnp.int32),
            dma((6,)),
            dma((2, 3, 2)),
            dma((2, 3, 2)),
            dma((7,)),
            dma((7,)),
            dma((2,)),
            dma((2,)),
            dma((7,)),
            dma((7,)),
            dma((4,)),
            dma((2,)),
        ],
        compiler_params=pltpu.CompilerParams(
            collective_id=0, has_side_effects=True, vmem_limit_bytes=VMEM_ALL
        ),
    )(near, basis, parent_basis, nbr, live)
    return pl.pallas_call(
        functools.partial(finish, n_leaf, n_col),
        out_shape=(
            jax.ShapeDtypeStruct((2, SK, NB * SK), F32),
            jax.ShapeDtypeStruct((4, SK, M), F32),
            jax.ShapeDtypeStruct((1, SK, SK), F32),
        ),
        in_specs=[hbm] * 4,
        out_specs=(hbm, hbm, vmem),
        scratch_shapes=[
            pltpu.VMEM((7, 128, 128), F32),
            pltpu.VMEM((M, M), F32),
            pltpu.VMEM((1, M, M), F32),
            pltpu.SMEM((2, NB), jnp.int32),
            pltpu.VMEM((2, NB, SK, SK), F32),
            pltpu.VMEM((2, SK, NB * SK), F32),
            dma((4,)),
            dma(()),
            dma((4,)),
        ],
        compiler_params=pltpu.CompilerParams(vmem_limit_bytes=VMEM_ALL),
    )(ring, joined, grand_basis, nbr)


def solution(mesh):
    both = ("leaf", "col")
    return jax.shard_map(
        functools.partial(on_device, mesh.shape["leaf"], mesh.shape["col"]),
        mesh=mesh,
        in_specs=(
            P(both, None, None, None),
            P(both, None, None),
            P("leaf", None, None),
            P("leaf", None, None),
            P(both, None),
            P(both, None),
            P(both, None),
        ),
        out_specs=(P(both, None, None), P("leaf", None, None), P("leaf", None, None)),
        check_vma=False,
    )
```

```python
import functools

import jax
import jax.numpy as jnp
from jax import lax
from jax.experimental import pallas as pl
from jax.experimental.pallas import tpu as pltpu
from jax.sharding import PartitionSpec as P

M = 256
SK = 64
RD = 192
NB = 13
G = 16
F32 = jnp.float32
HIGH = lax.Precision.HIGH
MESH = pl.DeviceIdType.MESH
VMEM_ALL = 67_000_000
NN = ((1,), (0,))
NT = ((1,), (1,))
TN = ((0,), (0,))


def mm(a, b, dims=NN):
    return lax.dot_general(a, b, (dims, ((), ())), precision=HIGH, preferred_element_type=F32)


def lane(x, k):
    return jnp.broadcast_to(x[:, k : k + 1], x.shape)


def sublane(x, k):
    return jnp.broadcast_to(x[k : k + 1, :], x.shape)


def tree_sum(terms):
    while len(terms) > 1:
        terms = [
            terms[i] + terms[i + 1] if i + 1 < len(terms) else terms[i]
            for i in range(0, len(terms), 2)
        ]
    return terms[0]


def forward_steps(rows_all, size, found):
    depth = G // 8
    row_ids = lax.broadcasted_iota(jnp.int32, (8, 128), 0)
    before, after = [], []
    for g in range(size // G):
        top, k0 = depth * g, G * g
        rows = list(rows_all[top : top + depth])
        before += rows
        following = range(top + depth, min(top + 2 * depth, size // 8))
        later = range(top + 2 * depth, size // 8)
        ahead = {u: [lane(rows_all[u], k0 + j) for j in range(G)] for u in following}
        cols = [[lane(rows[h], k0 + j) for h in range(depth)] for j in range(G)]
        scale = [None] * depth
        for k in range(G):
            kh, ks = divmod(k, 8)
            inverse = 1.0 / sublane(cols[k][kh], ks)
            here = row_ids == ks
            scale[kh] = inverse if ks == 0 else jnp.where(here, inverse, scale[kh])
            factor = [c * inverse for c in cols[k]]
            factor[kh] = jnp.where(here, 0.0, factor[kh])
            for j in range(k + 1, G):
                pivot = sublane(cols[j][kh], ks)
                cols[j] = [cols[j][h] - factor[h] * pivot for h in range(depth)]
            pivot = sublane(rows[kh], ks)
            rows = [rows[h] - factor[h] * pivot for h in range(depth)]
            yield
        rows = [rows[h] * scale[h] for h in range(depth)]
        after += rows
        for u in following:
            rows_all[u] = rows_all[u] - tree_sum(
                [ahead[u][j] * sublane(rows[j // 8], j % 8) for j in range(G)]
            )
        if later:
            left = jnp.concatenate([rows_all[u] for u in later], axis=0)[:, k0 : k0 + G]
            change = mm(left, jnp.concatenate(rows, axis=0))
            for n, u in enumerate(later):
                rows_all[u] = rows_all[u] - change[8 * n : 8 * n + 8]
    found.append((before, after))


def half_inverses(blocks):
    size = blocks[0].shape[0]
    r = lax.broadcasted_iota(jnp.int32, (size, size), 0)
    c = lax.broadcasted_iota(jnp.int32, (size, size), 1)
    eye = jnp.where(r == c, 1.0, 0.0).astype(F32)
    found, steps = [], []
    for block in blocks:
        wide = jnp.concatenate([block, eye], axis=1)
        mine = []
        found.append(mine)
        steps.append(
            forward_steps([wide[8 * i : 8 * i + 8] for i in range(size // 8)], size, mine)
        )
    going = True
    while going:
        for step in steps:
            if next(step, 0) == 0:
                going = False
    out = []
    for mine in found:
        before, after = mine[0]
        out.append(
            (
                jnp.concatenate(before, axis=0)[:, size:],
                jnp.concatenate(after, axis=0)[:, size:],
            )
        )
    return out


def eliminate(diags, bases, between=None):
    upper = [d[:RD] for d in diags]
    lower = list(bases)
    for b in range(3):
        halves = half_inverses([a[:SK, :SK] for a in upper])
        for i, (before, after) in enumerate(halves):
            a, e = upper[i], lower[i]
            z = mm(after, a[:SK, SK:])
            if b < 2:
                upper[i] = a[SK:, SK:] - mm(mm(a[SK:, :SK], before, NT), z)
            lower[i] = e[:, SK:] - mm(mm(e[:, :SK], before, NT), z)
        if between is not None and b < 2:
            between(b)
    return lower


def kernel(
    n_leaf,
    n_col,
    near_h,
    basis_h,
    pb_h,
    nbr_h,
    live_h,
    ring_o,
    joined_o,
    near_v,
    basis_v,
    pb_v,
    window,
    turned,
    sent,
    got,
    own_send,
    own_got,
    ring,
    joint,
    mixed,
    mixed_got,
    parts,
    share,
    shares,
    joined,
    nbr_s,
    live_s,
    load_sem,
    s_send,
    s_recv,
    f_send,
    f_recv,
    c_sem,
    m_sem,
    e_send,
    e_recv,
    r_sem,
    save_sem,
):
    total = n_leaf * n_col
    leaf_total = 2 * total
    row = lax.axis_index("leaf")
    col = lax.axis_index("col")
    me = row * n_col + col
    half = lax.rem(col, 2)
    parent = col // 2

    def place(k):
        n = lax.rem(me + k + total, total)
        return (n // n_col, lax.rem(n, n_col))

    partner = (row, col + 1 - 2 * half)

    loads = [
        pltpu.make_async_copy(nbr_h, nbr_s, load_sem.at[4]),
        pltpu.make_async_copy(live_h, live_s, load_sem.at[5]),
        pltpu.make_async_copy(basis_h, basis_v, load_sem.at[0]),
        pltpu.make_async_copy(near_h.at[:, 0], near_v.at[:, 0], load_sem.at[1]),
        pltpu.make_async_copy(near_h.at[:, 1:], near_v.at[:, 1:], load_sem.at[2]),
        pltpu.make_async_copy(pb_h, pb_v, load_sem.at[3]),
    ]
    for load in loads:
        load.start()
    barrier = pltpu.get_barrier_semaphore()
    for k in (1, -1, 2, -2, 3, -3):
        pl.semaphore_signal(barrier, inc=1, device_id=place(k), device_id_type=MESH)
    for k in range(1, n_col):
        pl.semaphore_signal(
            barrier, inc=1, device_id=(row, lax.rem(col + k, n_col)), device_id_type=MESH
        )

    loads[2].wait()
    for i in range(2):
        window[3, SK * i : SK * (i + 1), :] = basis_v[i, :, RD:].T

    def pass_on(step, side, j):
        source = 3 - step if side == 0 else 3 + step
        target = source - 1 if side == 0 else source + 1
        return pltpu.make_async_remote_copy(
            src_ref=window.at[source, pl.ds(SK * j, SK)],
            dst_ref=window.at[target, pl.ds(SK * j, SK)],
            send_sem=s_send.at[side, step, j],
            recv_sem=s_recv.at[side, step, j],
            device_id=place(1 if side == 0 else -1),
            device_id_type=MESH,
        )

    pl.semaphore_wait(barrier, 6 + n_col - 1)
    hops = [
        [pass_on(step, side, j) for j in range(2) for side in range(2)] for step in range(3)
    ]
    for hop in hops[0]:
        hop.start()
    flipped = [basis_v[i].T for i in range(2)]

    loads[3].wait()
    diags = []
    for i in range(2):
        t = mm(flipped[i], near_v[i, 0])
        turned[i, 3, SK * i : SK * (i + 1), :] = t[RD:, :]
        diags.append(mm(t, basis_v[i]))

    loads[0].wait()
    loads[1].wait()
    slots, lives = [], []
    for i in range(2):
        spots = []
        for q in range(NB):
            away = nbr_s[i, q] - (2 * me + i) + leaf_total + leaf_total // 2
            spot = lax.rem(away, leaf_total) - leaf_total // 2 + 6
            spots.append(jnp.clip(spot, 0, NB - 1))
        found, alive = [], []
        for o in range(NB):
            slot = jnp.int32(0)
            for q in range(1, NB):
                slot = jnp.where(spots[q] == o, q, slot)
            found.append(slot)
            alive.append(live_s[i, slot].astype(F32))
        slots.append((found, spots))
        lives.append(alive)

    loads[4].wait()

    def turn(e):
        for i in range(2):
            for j in range(2):
                o = 2 * (e - 3) + j - i + 6
                at = pl.ds(SK * j, SK)
                if o == 6:
                    continue
                if 0 <= o < NB:
                    turned[i, e, at, :] = (
                        mm(window[e, at, :], near_v[i, slots[i][0][o]]) * lives[i][o]
                    )
                else:
                    turned[i, e, at, :] = jnp.zeros((SK, M), F32)

    def relay(b):
        for hop, onward in zip(hops[b], hops[b + 1]):
            hop.wait_recv()
            onward.start()

    def early(b):
        if b == 1:
            relay(0)
            turn(3)
            turn(2)
            turn(4)

    weights = eliminate(diags, [basis_v[0], basis_v[1]], early)

    v, vt = [], []
    for i in range(2):
        v.append(weights[i] - 0.5 * basis_v[i, :, RD:])
        vt.append(v[i].T)

    def send(e):
        return pltpu.make_async_remote_copy(
            src_ref=sent.at[e],
            dst_ref=got.at[6 - e],
            send_sem=f_send.at[e],
            recv_sem=f_recv.at[6 - e],
            device_id=place(e - 3),
            device_id_type=MESH,
        )

    def out_and_mine(e):
        sent[e] = jnp.concatenate([mm(turned[i, e], v[i]) for i in range(2)], axis=1)
        for i in range(2):
            ring[e + 4, SK * i : SK * (i + 1), :] = mm(vt[i], turned[i, e], NT)

    sends = {e: send(e) for e in range(7) if e != 3}
    out_and_mine(3)
    mine = ring[7] + sent[3]
    for i in range(2):
        at = slice(SK * i, SK * (i + 1))
        own_send[at, :] = mine[at, :]
        own_send[at, at] = mm(turned[i, 3, at, :], weights[i])
    ring[7] = own_send[...]
    own_copy = pltpu.make_async_remote_copy(
        src_ref=own_send,
        dst_ref=own_got,
        send_sem=c_sem.at[0],
        recv_sem=c_sem.at[1],
        device_id=partner,
        device_id_type=MESH,
    )
    own_copy.start()
    for e in (2, 4):
        out_and_mine(e)
        sends[e].start()
    relay(1)
    for e in (1, 5):
        turn(e)
        out_and_mine(e)
        sends[e].start()
    for hop in hops[2]:
        hop.wait_recv()
    for e in (0, 6):
        turn(e)
        out_and_mine(e)
        sends[e].start()

    for e in range(4):
        ring[e] = jnp.zeros((128, 128), F32)
        ring[e + 11] = jnp.zeros((128, 128), F32)
    loads[5].wait()
    pb_own = pb_v[parent]
    pb_flip = pb_own.T
    own_copy.wait_recv()
    for e in (2, 4):
        sends[6 - e].wait_recv()
        ring[e + 4] += got[e]
    cross = ring[8 - 2 * half]
    here = pl.multiple_of(half * 128, 128)
    there = pl.multiple_of(128 - half * 128, 128)
    joint[pl.ds(here, 128), pl.ds(here, 128)] = own_send[...]
    joint[pl.ds(there, 128), pl.ds(there, 128)] = own_got[...]
    joint[pl.ds(here, 128), pl.ds(there, 128)] = cross
    joint[pl.ds(there, 128), pl.ds(here, 128)] = cross.T
    diag = mm(mm(pb_flip, joint[...]), pb_own)

    mixed_copy = pltpu.make_async_remote_copy(
        src_ref=mixed.at[1 - half],
        dst_ref=mixed_got,
        send_sem=m_sem.at[0],
        recv_sem=m_sem.at[1],
        device_id=partner,
        device_id_type=MESH,
    )

    def mix(b):
        if b != 1:
            return
        for e in (1, 5, 0, 6):
            sends[6 - e].wait_recv()
            ring[e + 4] += got[e]
        for u in range(4):
            skel = pb_v[u, :, RD:]
            mixed[u // 2, :, SK * (u % 2) : SK * (u % 2 + 1)] = mm(
                ring[2 * u + 7 - col], skel[:128]
            ) + mm(ring[2 * u + 8 - col], skel[128:])
        mixed_copy.start()

    (w,) = eliminate([diag], [pb_own], mix)
    parts[...] = jnp.concatenate([w - 0.5 * pb_own[:, RD:], 0.5 * w], axis=1)
    mixed_copy.wait_recv()
    both = mm(parts[pl.ds(here, 128), :], mixed[half], TN) + mm(
        parts[pl.ds(there, 128), :], mixed_got[...], TN
    )
    of = lax.broadcasted_iota(jnp.int32, (SK, 128), 1) // SK + 2 * half
    piece = jnp.where(of == parent, both[SK:], both[:SK])
    share[...] = piece
    spreads = []
    for k in range(1, n_col):
        spreads.append(
            pltpu.make_async_remote_copy(
                src_ref=share,
                dst_ref=shares.at[col],
                send_sem=e_send.at[k - 1],
                recv_sem=e_recv.at[k - 1],
                device_id=(row, lax.rem(col + k, n_col)),
                device_id_type=MESH,
            )
        )
    for k in (4, 3, 5, 2, 6, 1, 7):
        spreads[k - 1].start()
    shares[col] = piece
    ring_save = pltpu.make_async_copy(ring.at[4:11], ring_o, save_sem.at[0])
    ring_save.start()

    for k in range(1, n_col):
        pltpu.make_async_remote_copy(
            src_ref=share,
            dst_ref=shares.at[lax.rem(col - k + n_col, n_col)],
            send_sem=e_send.at[k - 1],
            recv_sem=e_recv.at[k - 1],
            device_id=(row, lax.rem(col + k, n_col)),
            device_id_type=MESH,
        ).wait_recv()
    rows = [jnp.concatenate([shares[2 * p], shares[2 * p + 1]], axis=1) for p in range(4)]
    summed = jnp.concatenate(rows, axis=0)
    joined[...] = summed + summed.T
    joined_save = pltpu.make_async_copy(joined, joined_o, save_sem.at[1])
    joined_save.start()

    for step in range(3):
        for hop in hops[step]:
            hop.wait_send()
    for e in sends:
        sends[e].wait_send()
    own_copy.wait_send()
    mixed_copy.wait_send()
    for spread in spreads:
        spread.wait_send()
    ring_save.wait()
    joined_save.wait()


def finish(
    n_leaf,
    n_col,
    ring_h,
    joined_h,
    gb_h,
    nbr_h,
    leaf_o,
    par_o,
    top_o,
    ring,
    joined,
    gb_v,
    nbr_s,
    blocks,
    leaf_v,
    load_sem,
    leaf_sem,
    par_sem,
):
    leaf_total = 2 * n_leaf * n_col
    me = lax.axis_index("leaf") * n_col + lax.axis_index("col")
    loads = [
        pltpu.make_async_copy(gb_h, gb_v, load_sem.at[0]),
        pltpu.make_async_copy(joined_h, joined, load_sem.at[1]),
        pltpu.make_async_copy(nbr_h, nbr_s, load_sem.at[2]),
        pltpu.make_async_copy(ring_h, ring, load_sem.at[3]),
    ]
    for load in loads:
        load.start()
    loads[0].wait()
    loads[1].wait()
    saves = [
        pltpu.make_async_copy(joined.at[pl.ds(SK * p, SK)], par_o.at[p], par_sem.at[p])
        for p in range(4)
    ]
    for save in saves:
        save.start()
    def tidy(b):
        if b:
            return
        loads[2].wait()
        loads[3].wait()
        for e in range(7):
            whole = ring[e]
            for i in range(2):
                for j in range(2):
                    o = 2 * (e - 3) + j - i + 6
                    if 0 <= o < NB:
                        blocks[i, o] = whole[SK * i : SK * (i + 1), SK * j : SK * (j + 1)]
        for i in range(2):
            for q in range(NB):
                away = nbr_s[i, q] - (2 * me + i) + leaf_total + leaf_total // 2
                spot = lax.rem(away, leaf_total) - leaf_total // 2 + 6
                leaf_v[i, :, SK * q : SK * (q + 1)] = blocks[i, jnp.clip(spot, 0, NB - 1)]
        saves.append(pltpu.make_async_copy(leaf_v, leaf_o, leaf_sem))
        saves[-1].start()

    gb = gb_v[0]
    t = mm(gb.T, joined[...])
    (w,) = eliminate([mm(t, gb)], [gb], tidy)
    top_o[0] = mm(t[RD:], w)
    for save in saves:
        save.wait()


def on_device(n_leaf, n_col, near, basis, parent_basis, grand_basis, nbr, live, partner):
    hbm = pl.BlockSpec(memory_space=pltpu.HBM)
    vmem = pl.BlockSpec(memory_space=pltpu.VMEM)
    dma = pltpu.SemaphoreType.DMA
    ring, joined = pl.pallas_call(
        functools.partial(kernel, n_leaf, n_col),
        out_shape=(
            jax.ShapeDtypeStruct((7, 128, 128), F32),
            jax.ShapeDtypeStruct((M, M), F32),
        ),
        in_specs=[hbm] * 5,
        out_specs=(hbm, hbm),
        scratch_shapes=[
            pltpu.VMEM((2, NB, M, M), F32),
            pltpu.VMEM((2, M, M), F32),
            pltpu.VMEM((4, M, M), F32),
            pltpu.VMEM((7, 128, M), F32),
            pltpu.VMEM((2, 7, 128, M), F32),
            pltpu.VMEM((7, 128, 128), F32),
            pltpu.VMEM((7, 128, 128), F32),
            pltpu.VMEM((128, 128), F32),
            pltpu.VMEM((128, 128), F32),
            pltpu.VMEM((15, 128, 128), F32),
            pltpu.VMEM((M, M), F32),
            pltpu.VMEM((2, 128, 128), F32),
            pltpu.VMEM((128, 128), F32),
            pltpu.VMEM((M, 128), F32),
            pltpu.VMEM((SK, 128), F32),
            pltpu.VMEM((8, SK, 128), F32),
            pltpu.VMEM((M, M), F32),
            pltpu.SMEM((2, NB), jnp.int32),
            pltpu.SMEM((2, NB), jnp.int32),
            dma((6,)),
            dma((2, 3, 2)),
            dma((2, 3, 2)),
            dma((7,)),
            dma((7,)),
            dma((2,)),
            dma((2,)),
            dma((7,)),
            dma((7,)),
            dma((4,)),
            dma((2,)),
        ],
        compiler_params=pltpu.CompilerParams(
            collective_id=0, has_side_effects=True, vmem_limit_bytes=VMEM_ALL
        ),
    )(near, basis, parent_basis, nbr, live)
    return pl.pallas_call(
        functools.partial(finish, n_leaf, n_col),
        out_shape=(
            jax.ShapeDtypeStruct((2, SK, NB * SK), F32),
            jax.ShapeDtypeStruct((4, SK, M), F32),
            jax.ShapeDtypeStruct((1, SK, SK), F32),
        ),
        in_specs=[hbm] * 4,
        out_specs=(hbm, hbm, vmem),
        scratch_shapes=[
            pltpu.VMEM((7, 128, 128), F32),
            pltpu.VMEM((M, M), F32),
            pltpu.VMEM((1, M, M), F32),
            pltpu.SMEM((2, NB), jnp.int32),
            pltpu.VMEM((2, NB, SK, SK), F32),
            pltpu.VMEM((2, SK, NB * SK), F32),
            dma((4,)),
            dma(()),
            dma((4,)),
        ],
        compiler_params=pltpu.CompilerParams(vmem_limit_bytes=VMEM_ALL),
    )(ring, joined, grand_basis, nbr)


def solution(mesh):
    both = ("leaf", "col")
    return jax.shard_map(
        functools.partial(on_device, mesh.shape["leaf"], mesh.shape["col"]),
        mesh=mesh,
        in_specs=(
            P(both, None, None, None),
            P(both, None, None),
            P("leaf", None, None),
            P("leaf", None, None),
            P(both, None),
            P(both, None),
            P(both, None),
        ),
        out_specs=(P(both, None, None), P("leaf", None, None), P("leaf", None, None)),
        check_vma=False,
    )
```
